128 devices in a mesh: ep: 64 (over z, y, x_hi, core), dp: 2 (over x_lo).
Axes of the slice: x: 4 (x_hi: 2, x_lo: 2; x = x_hi * 2 + x_lo), y: 4, z: 4, core: 2. Of those that a mesh axis runs over, the one named last changes fastest.
Arguments:
- hidden: bfloat16 [3, 2048, 4096], P(None, ('dp', 'ep')), parts along dimension 1, may hold values from -6 to 6
- expert_ids: int32 [3, 2048, 8], P(None, ('dp', 'ep')), parts along dimension 1, may hold values from 0 to 63, all different within a row; in each aligned block of 16 rows (0 to 15, 16 to 31, ..., all dimensions but the last counted through in order) at most 5 rows name the same one
- gate_logits: float32 [3, 2048, 8], P(None, ('dp', 'ep')), parts along dimension 1, may hold values from -2 to 2
- w_gate_up: bfloat16 [64, 4096, 1536], P('ep'), may hold values from -0.09375 to 0.09375
- w_down: bfloat16 [64, 768, 4096], P('ep'), may hold values from -0.21875 to 0.21875
- swap_step: int32 [128], P('dp'), parts along dimension 0, may hold values from 1 to 3, as said below
Outputs:
- mixed: bfloat16 [3, 2048, 4096], P(None, ('dp', 'ep')), parts along dimension 1
- relocated_down: bfloat16 [128, 768, 4096], P(('dp', 'ep')), parts along dimension 0
The draws below stay inside these ranges and needn't reach their ends.
There are 2 independent parts, one for each index of `dp`. The reference program is written for one: setup_inputs(seed, part) draws one part's arguments, and reference() takes and returns one part's arrays. A program takes and returns all parts, laid end to end along the dimension named above; an argument that names none is the same for every part. Nothing has to cross between parts.
Inputs may be any that keep to these rules, and one draw needn't show every extreme that they name: `expert_ids`: each token names 8 different experts; within one step, the 16 tokens of one device (aligned blocks) name one expert in at most 5 of their rows, and some expert in exactly 5 rows in some blocks. `swap_step`: slots 2i and 2i+1 share one value; 3 means the pair keeps its experts through the steps.
All inputs are finite; a program needn't handle non-finite values.
Results may differ from the reference program's by a relative error of at most 0.0057.
Values may be sent and summed in bfloat16 or wider, within the bound.
A program may use at most 192 MiB of HBM per device.

```python
import math
import jax
import jax.numpy as jnp
import numpy as np
from jax import lax

D = 4096
TOPK = 8
FFW = 768
TOK_DEV = 16
STEPS = 3
EXPERTS = 64
TOKENS = 1024
CAP = 5
N_EP = 64


def draw_swap_step(key, part):
    pair_count = EXPERTS // 2
    values = jax.random.randint(jax.random.fold_in(key, 3), (pair_count,), 1, STEPS + 1)
    values = values.at[0].set(1).at[1].set(STEPS)
    return jnp.repeat(values, 2).astype(jnp.int32)


def block_scale(key, extent, split, low, top_value):
    loudness, own = 1.0, jax.random.fold_in(key, 6)
    for position, shards_of in split:
        draws = jnp.exp(jax.random.uniform(jax.random.fold_in(own, position), (shards_of,), jnp.float32, low / len(split), top_value / len(split)))
        loudness = loudness * jnp.repeat(draws, extent[position] // shards_of).reshape([-1 if axis == position else 1 for axis in range(len(extent))])
    return loudness


def deal_out(key, own, number, rows, amount, top, bound, skew):
    ranking = jax.random.permutation(key, amount)
    crowded, usual = portions_of(amount, rows * top, bound, skew, True), portions_of(amount, rows * top, bound, skew, False)
    places = jnp.arange(amount)

    def named(tallies, turn):
        used = int((tallies > 0).sum())
        fixed = max(1, used // 4)
        shifted = fixed + (places - fixed + turn * (used - fixed)) % max(1, amount - fixed)
        return jnp.zeros((amount,), jnp.int32).at[ranking[jnp.where(places < fixed, places, shifted)]].set(jnp.asarray(tallies, jnp.int32))

    tallies = jnp.where(number % 4 == 0, named(crowded, number // 4), named(usual, number - number // 4 - 1))
    mixed = jax.random.permutation(jax.random.fold_in(own, 3), amount)
    source_of, receiver = mixed[0:amount // 2 * 2:2], mixed[1:amount // 2 * 2:2]
    margin = jnp.minimum(tallies[source_of] - 1, bound - tallies[receiver]) // 2
    margin = jnp.where((source_of == ranking[0]) | (receiver == ranking[0]) | (tallies[receiver] == 0), 0, jnp.maximum(margin, 0))
    shifted = jax.random.randint(jax.random.fold_in(own, 4), (amount // 2,), 0, 1 << 20) % (margin + 1)
    tallies = tallies.at[source_of].add(-shifted).at[receiver].add(shifted)
    members = jnp.searchsorted(jnp.cumsum(tallies), jnp.arange(rows * top), side="right").astype(jnp.int32)
    listing = members.reshape(top, rows).T
    listing = listing[jax.random.permutation(jax.random.fold_in(own, 1), rows)]
    turn = jax.random.randint(jax.random.fold_in(own, 2), (rows, 1), 0, top)
    return jnp.take_along_axis(listing, (jnp.arange(top)[None, :] + turn) % top, axis=1)


def portions_of(number_of, total, reach, slope, full):
    weights = [(1 << 20) // math.isqrt(grade ** slope) + 1 for grade in range(1, number_of + 1)]
    largest = reach if full else min(reach, max(-(-total // number_of), total * weights[0] // sum(weights)))
    least = 1 if total - largest >= number_of - 1 else 0
    counts, surplus = [largest] + [least] * (number_of - 1), total - largest - least * (number_of - 1)
    while surplus > 0:
        movable = [i for i in range(1, number_of) if counts[i] < largest] or [i for i in range(1, number_of) if counts[i] < reach]
        pool, remaining = sum([weights[i] for i in movable]), surplus
        for i in movable:
            addition = min(reach - counts[i], max(1, remaining * weights[i] // pool), surplus)
            counts[i] = counts[i] + addition
            surplus = surplus - addition
    return np.array(counts)


def noise(rng, shape, spread, reach, pieces=(), kind=jnp.bfloat16):
    result = jax.random.normal(rng, shape, jnp.float32) * spread
    if len(pieces) > 0:
        result = block_scale(rng, shape, pieces, -0.22, 0.18) * result
    return jnp.clip(result, min=-reach, max=reach).astype(kind)


def setup_inputs(seed: int = 0, part: int = 0) -> dict:
    key_of = jax.random.split(jax.random.key(seed), 7)
    part_splits = jax.random.split(jax.random.fold_in(key_of[6], part), 7)
    hidden = noise(part_splits[0], (STEPS, TOKENS, D), 1.0, 6.0, ((1, 64),))
    expert_ids_keys = jax.random.split(jax.random.fold_in(part_splits[1], 1), STEPS * TOKENS // TOK_DEV)
    expert_ids_turns = jax.random.permutation(jax.random.fold_in(part_splits[1], 3), STEPS * TOKENS // TOK_DEV)
    expert_ids = jax.vmap(lambda own, number: deal_out(jax.random.fold_in(part_splits[1], 2), own, number, TOK_DEV, EXPERTS, TOPK, CAP, 2))(expert_ids_keys, expert_ids_turns).reshape((STEPS, TOKENS, TOPK))
    gate_logits = jnp.clip(jax.random.uniform(part_splits[2], (STEPS, TOKENS, TOPK), jnp.float32, -2.0, 2.0) * block_scale(part_splits[2], (STEPS, TOKENS, TOPK), ((1, 64),), -0.4, 0.0), -2.0, 2.0)
    w_gate_up = noise(key_of[3], (EXPERTS, D, 2 * FFW), D ** -0.5, 0.09375, ((0, 64),))
    w_down = noise(key_of[4], (EXPERTS, FFW, D), FFW ** -0.5, 0.21875, ((0, 64),))
    swap_step = draw_swap_step(jax.random.fold_in(jax.random.fold_in(key_of[6], part), 71), part)
    return dict(hidden=hidden, expert_ids=expert_ids, gate_logits=gate_logits, w_gate_up=w_gate_up, w_down=w_down, swap_step=swap_step)


def expert_rows(rows_in, gate_up, down_proj):
    product = jnp.dot(rows_in, gate_up, preferred_element_type=jnp.float32)
    activated = (jax.nn.silu(product[:, :FFW]) * product[:, FFW:]).astype(jnp.bfloat16)
    return jnp.dot(activated, down_proj, preferred_element_type=jnp.float32).astype(jnp.bfloat16)


def reference(hidden, expert_ids, gate_logits, w_gate_up, w_down, swap_step):
    row_bound = N_EP * CAP
    results = []
    for step_idx in range(STEPS):
        step_rows = hidden[step_idx]
        flat_ids = expert_ids[step_idx].reshape(-1)
        exponent = jnp.exp(gate_logits[step_idx])
        gate_weights = (exponent / jnp.sum(exponent, axis=-1, keepdims=True)).reshape(-1)

        def add_expert(total, item):
            expert, gate_up, down_proj = item
            matches = flat_ids == expert
            selected = jnp.nonzero(matches, size=row_bound, fill_value=0)[0]
            row_count = jnp.sum(matches.astype(jnp.int32))
            is_valid = jnp.arange(row_bound) < row_count
            tokens = selected // TOPK
            expert_out = expert_rows(step_rows[tokens], gate_up, down_proj).astype(jnp.float32)
            weight = jnp.where(is_valid, gate_weights[selected], jnp.zeros_like(gate_weights[selected]))
            return total.at[tokens].add(expert_out * weight[:, None]), None

        total, _ = lax.scan(add_expert, jnp.zeros((TOKENS, D), jnp.float32),
                            (jnp.arange(EXPERTS, dtype=jnp.int32), w_gate_up, w_down))
        results.append(total.astype(jnp.bfloat16))
    mixed = jnp.stack(results)
    expert_index = jnp.arange(EXPERTS, dtype=jnp.int32)
    partner = expert_index + 1 - 2 * (expert_index % 2)
    source = jnp.where(swap_step < STEPS, partner, expert_index)
    return mixed, w_down[source]
```

```python
import jax
import jax.numpy as jnp
from jax import lax
from jax.sharding import PartitionSpec as P

CAP = 5


def expert_block(rows_in, gate_up, down_proj):
    hidden_width = down_proj.shape[0]
    product = jnp.dot(rows_in, gate_up, preferred_element_type=jnp.float32)
    activated = (jax.nn.silu(product[:, :hidden_width]) * product[:, hidden_width:]).astype(
        jnp.bfloat16
    )
    return jnp.dot(activated, down_proj, preferred_element_type=jnp.float32).astype(jnp.bfloat16)


def routing(expert_ids, gate_logits, devices, slots):
    num_steps, tok_rows, _ = expert_ids.shape
    exponent = jnp.exp(gate_logits)
    weights = exponent / jnp.sum(exponent, axis=-1, keepdims=True)
    match = expert_ids[..., None] == jnp.arange(devices, dtype=jnp.int32)
    names = jnp.any(match, axis=2)
    dense_weight = jnp.sum(jnp.where(match, weights[..., None], 0.0), axis=2)
    earlier = jnp.arange(tok_rows)[:, None] > jnp.arange(tok_rows)[None, :]
    rank = jnp.sum(
        (earlier[None, :, :, None] & names[:, None, :, :]).astype(jnp.int32), axis=2
    )
    slot = rank + CAP * jnp.arange(num_steps, dtype=jnp.int32)[:, None, None]
    slot = jnp.where(names, slot, -1).reshape(num_steps * tok_rows, devices)
    onehot = slot[:, :, None] == jnp.arange(slots, dtype=jnp.int32)
    weighted = jnp.where(
        onehot, dense_weight.reshape(num_steps * tok_rows, devices)[:, :, None], 0.0
    )
    rows = num_steps * tok_rows
    return (
        onehot.astype(jnp.bfloat16).reshape(rows, devices * slots),
        weighted.reshape(rows, devices * slots),
    )


def on_device(hidden, expert_ids, gate_logits, w_gate_up, w_down, swap_step):
    devices = lax.axis_size("ep")
    my_index = lax.axis_index("ep")
    num_steps, tok_rows, model_dim = hidden.shape
    slots = 16
    pairs = [(source, source ^ 1) for source in range(devices)]
    other_down = lax.ppermute(w_down[0], "ep", pairs)
    onehot, weighted = routing(expert_ids, gate_logits, devices, slots)
    tokens = hidden.reshape(num_steps * tok_rows, model_dim)
    send = lax.dot_general(
        onehot, tokens, (((0,), (0,)), ((), ())), preferred_element_type=jnp.float32
    ).astype(jnp.bfloat16)
    received = lax.all_to_all(
        send.reshape(devices, slots, model_dim), "ep", split_axis=0, concat_axis=0, tiled=True
    )
    outputs = expert_block(
        received.reshape(devices * slots, model_dim), w_gate_up[0], w_down[0]
    )
    returned = lax.all_to_all(
        outputs.reshape(devices, slots, model_dim), "ep", split_axis=0, concat_axis=0, tiled=True
    ).reshape(devices * slots, model_dim)
    high = weighted.astype(jnp.bfloat16)
    low = (weighted - high.astype(jnp.float32)).astype(jnp.bfloat16)
    both = jnp.dot(
        jnp.concatenate([high, low], axis=0), returned, preferred_element_type=jnp.float32
    )
    rows = num_steps * tok_rows
    mixed = (both[:rows] + both[rows:]).astype(jnp.bfloat16).reshape(hidden.shape)
    relocated = jnp.where(swap_step[my_index] < num_steps, other_down, w_down[0])
    return (mixed, relocated[None])


def solution(mesh):
    in_specs = (
        P(None, ("dp", "ep"), None),
        P(None, ("dp", "ep"), None),
        P(None, ("dp", "ep"), None),
        P("ep", None, None),
        P("ep", None, None),
        P("dp"),
    )
    out_specs = (P(None, ("dp", "ep"), None), P(("dp", "ep"), None, None))
    return jax.shard_map(
        on_device, mesh=mesh, in_specs=in_specs, out_specs=out_specs, check_vma=False
    )
```

```python
import functools

import jax
import jax.numpy as jnp
from jax import lax
from jax.experimental import pallas as pl
from jax.experimental.pallas import tpu as pltpu
from jax.sharding import PartitionSpec as P

CAP = 5
STEPS = 3
TOK = 16
RING = 4
BLOCKS = 32
GROUP = 16
META = 128
OWN, OTHER = 0, 1
UP, DOWN = 0, 1
OFFSETS = (0, 3, 1, 2)
BF16 = jnp.bfloat16
F32 = jnp.float32


def moe_kernel(
    expert_ref, tok_a, tok_b, wgu_hbm, wd_hbm, out_ref,
    gath_a, gath_b, rbuf_a, rbuf_b, wgu, wd, picked, pick_send, out_own, out_send, out_recv,
    act, weight_hi, weight_lo,
    ag_send, ag_recv, rs_send, rs_recv, pair_send, pair_recv, load_sem,
):
    half = tok_b.shape[1]
    hidden_width = wd.shape[0]
    gath = (gath_a, gath_b)
    rbuf = (rbuf_a, rbuf_b)
    tok = (tok_a, tok_b)
    me = lax.axis_index("ep")
    my_dp = lax.axis_index("dp")
    core = me % 2
    xh = (me // 2) % 2
    y = (me // 4) % RING
    z = me // 16

    def device(zz, yy, xx, dp):
        return {"ep": ((zz * RING + yy) * 2 + xx) * 2 + core, "dp": dp}

    x_partner = device(z, y, 1 - xh, 1 - my_dp)
    core_partner = {"ep": me + 1 - 2 * core, "dp": my_dp}
    first = (z, y)
    second = (y, z)

    def place(h, f, g):
        return (f, g) if h == 0 else (g, f)

    def block(h, f, g, kind):
        zz, yy = place(h, f, g)
        xx = xh if kind == OWN else 1 - xh
        start = ((zz * RING + yy) * 2 + xx) * TOK
        return pl.ds(pl.multiple_of(start, TOK), TOK)

    def shifted(value, amount):
        return (value + amount) % RING

    def first_to(h, way):
        f = shifted(first[h], 1 if way == UP else 3)
        zz, yy = place(h, f, second[h])
        return device(zz, yy, xh, my_dp)

    def second_to(h, way):
        g = shifted(second[h], 1 if way == UP else 3)
        zz, yy = place(h, first[h], g)
        return device(zz, yy, xh, my_dp)

    def remote(src, dst, send, recv, to):
        return pltpu.make_async_remote_copy(
            src_ref=src, dst_ref=dst, send_sem=send, recv_sem=recv,
            device_id=to, device_id_type=pl.DeviceIdType.MESH,
        )

    loads = (
        pltpu.make_async_copy(wgu_hbm, wgu, load_sem.at[0]),
        pltpu.make_async_copy(wd_hbm, wd, load_sem.at[1]),
    )

    barrier = pltpu.get_barrier_semaphore()
    friends = [x_partner, core_partner] + [
        to(0, way) for to in (first_to, second_to) for way in (UP, DOWN)
    ]
    for friend in friends:
        pl.semaphore_signal(
            barrier, inc=1, device_id=friend, device_id_type=pl.DeviceIdType.MESH
        )
    pl.semaphore_wait(barrier, len(friends))

    ag_started = {}

    def ag_copy(h, s, idx, rows, to, from_input=False):
        source = (
            tok[h].at[pl.ds(s * TOK, TOK), :] if from_input else gath[h].at[s, rows, :]
        )
        return remote(
            source, gath[h].at[s, rows, :], ag_send.at[h, s, idx], ag_recv.at[h, s, idx], to
        )

    def ag_start(h, s, idx, rows, to, from_input=False):
        copy = ag_copy(h, s, idx, rows, to, from_input)
        copy.start()
        ag_started.setdefault(s, []).append(copy)

    def ag_wait(h, s, idx, rows):
        ag_copy(h, s, idx, rows, x_partner).wait_recv()

    def ag_actions(h, s):
        f, g = first[h], second[h]
        f_of = [shifted(f, off) for off in OFFSETS]

        def spread(j, kind, from_input=False):
            for way in (UP, DOWN):
                ag_start(
                    h, s, 7 + way * 8 + j * 2 + kind, block(h, f_of[j], g, kind),
                    second_to(h, way), from_input,
                )

        def init():
            mine = block(h, f, g, OWN)
            ag_start(h, s, 0, mine, x_partner, True)
            for way in (UP, DOWN):
                ag_start(h, s, 1 + way * 2 + OWN, mine, first_to(h, way), True)
            gath[h][s, mine, :] = tok[h][pl.ds(s * TOK, TOK), :]

        def init2():
            spread(0, OWN, True)

        def a1():
            theirs = block(h, f, g, OTHER)
            ag_wait(h, s, 0, theirs)
            for way in (UP, DOWN):
                ag_start(h, s, 1 + way * 2 + OTHER, theirs, first_to(h, way))
            spread(0, OTHER)

        def near(way, kind):
            j = 1 if way == UP else 2
            rows = block(h, f_of[j], g, kind)
            ag_wait(h, s, 1 + way * 2 + kind, rows)
            if (way, kind) == (UP, OWN) or (way, kind) == (DOWN, OTHER):
                ag_start(h, s, 5 + way, rows, first_to(h, way))
            spread(j, kind)

        def far(way):
            kind = OWN if way == UP else OTHER
            ag_wait(h, s, 5 + way, block(h, f_of[3], g, kind))
            spread(3, kind)

        def forward(j, kind):
            way = UP if kind == OWN else DOWN
            rows = block(h, f_of[j], shifted(g, 3 if way == UP else 1), kind)
            ag_wait(h, s, 7 + way * 8 + j * 2 + kind, rows)
            ag_start(h, s, 23 + way * 4 + j, rows, second_to(h, way))

        def last(j):
            ag_wait(h, s, 7 + DOWN * 8 + j * 2 + OWN, block(h, f_of[j], shifted(g, 1), OWN))
            ag_wait(h, s, 7 + UP * 8 + j * 2 + OTHER, block(h, f_of[j], shifted(g, 3), OTHER))
            ag_wait(h, s, 23 + UP * 4 + j, block(h, f_of[j], shifted(g, 2), OWN))
            ag_wait(h, s, 23 + DOWN * 4 + j, block(h, f_of[j], shifted(g, 2), OTHER))

        part = functools.partial
        head = [init, init2]
        body = [
            a1, part(near, UP, OWN), part(near, DOWN, OWN), part(forward, 0, OWN),
            part(near, UP, OTHER), part(near, DOWN, OTHER), part(forward, 0, OTHER),
            part(far, UP), part(far, DOWN),
            part(forward, 1, OWN), part(forward, 2, OWN),
            part(forward, 1, OTHER), part(forward, 2, OTHER),
            part(forward, 3, OWN), part(forward, 3, OTHER),
        ]
        tail = [part(last, j) for j in (0, 1, 2, 3)]
        return head, body, tail

    def both(make, s):
        a, b = make(0, s), make(1, s)
        return [
            [act_ for pair in zip(pa, pb) for act_ in pair] for pa, pb in zip(a, b)
        ]

    chunk = min(512, half)
    act_chunk = min(256, hidden_width)

    def routing(s, grp):
        meta = gath_a[s, pl.ds(grp * 256, 256), pl.ds(half, META)].astype(F32)
        lane = lax.broadcasted_iota(jnp.int32, (256, META), 1)
        row = lax.broadcasted_iota(jnp.int32, (256, 256), 0)
        col = lax.broadcasted_iota(jnp.int32, (256, 256), 1)
        lower = jnp.where(
            (row > col) & (row // TOK == col // TOK), 1.0, 0.0
        ).astype(BF16)
        base = ((row // TOK) * CAP).astype(F32)
        colf = col.astype(F32)
        slot = jnp.zeros((256, 256), F32)
        hi = jnp.zeros((256, 256), F32)
        lo = jnp.zeros((256, 256), F32)
        shifted_hi = pltpu.roll(meta, META - 8, axis=1)
        shifted_lo = pltpu.roll(meta, META - 16, axis=1)
        for kind in (0, 1):
            expert = expert_ref[kind]
            match = (meta == expert) & (lane < 8)
            names = jnp.sum(jnp.where(match, 1.0, 0.0), axis=1, keepdims=True)
            w_hi = jnp.sum(jnp.where(match, shifted_hi, 0.0), axis=1, keepdims=True)
            w_lo = jnp.sum(jnp.where(match, shifted_lo, 0.0), axis=1, keepdims=True)
            rank = jnp.dot(
                lower, jnp.broadcast_to(names, (256, 256)).astype(BF16),
                preferred_element_type=F32,
            )
            target = base + rank + float(kind * GROUP * CAP)
            here = jnp.where((colf == target) & (names > 0.5), 1.0, 0.0)
            slot += here
            hi += here * w_hi
            lo += here * w_lo
        weight_hi[grp] = hi.astype(BF16)
        weight_lo[grp] = lo.astype(BF16)
        return slot.T.astype(BF16)[: 2 * GROUP * CAP, :]

    group_rows = GROUP * CAP
    own_rows = 2 * group_rows

    def select(s, grp):
        onehot = routing(s, grp)
        for h in (0, 1):
            for c in range(half // chunk):
                got = jnp.dot(
                    onehot,
                    gath[h][s, pl.ds(grp * 256, 256), pl.ds(c * chunk, chunk)],
                    preferred_element_type=F32,
                ).astype(BF16)
                at = pl.ds(h * half + c * chunk, chunk)
                picked[s, pl.ds(grp * group_rows, group_rows), at] = got[:group_rows]
                pick_send[s % 2, pl.ds(grp * group_rows, group_rows), at] = got[group_rows:]

    def pick_copy(s):
        return remote(
            pick_send.at[s % 2], picked.at[s, pl.ds(own_rows, own_rows), :],
            pair_send.at[0, s], pair_recv.at[0, s], core_partner,
        )

    def back_copy(s):
        return remote(
            out_send.at[s % 2], out_recv.at[s], pair_send.at[1, s], pair_recv.at[1, s],
            core_partner,
        )

    def ffn_up(s, c):
        rows = picked[s]
        gate = jnp.dot(rows, wgu[:, pl.ds(c * act_chunk, act_chunk)], preferred_element_type=F32)
        up = jnp.dot(
            rows, wgu[:, pl.ds(hidden_width + c * act_chunk, act_chunk)],
            preferred_element_type=F32,
        )
        act[:, pl.ds(c * act_chunk, act_chunk)] = (
            gate / (1.0 + jnp.exp(-gate)) * up
        ).astype(BF16)

    def ffn_down(s, c):
        at = pl.ds(c * chunk, chunk)
        got = jnp.dot(act[...], wd[:, at], preferred_element_type=F32).astype(BF16)
        out_own[:, at] = got[:own_rows]
        out_send[s % 2, :, at] = got[own_rows:]

    def partial_sums(s, grp, c):
        rows = pl.ds(grp * group_rows, group_rows)
        h, offset = divmod(c * chunk, half)
        at = pl.ds(c * chunk, chunk)
        outs = jnp.concatenate([out_own[rows, at], out_recv[s, rows, at]], axis=0)
        total = jnp.dot(
            weight_hi[grp, :, : 2 * group_rows], outs, preferred_element_type=F32
        ) + jnp.dot(weight_lo[grp, :, : 2 * group_rows], outs, preferred_element_type=F32)
        gath[h][s, pl.ds(grp * 256, 256), pl.ds(offset, chunk)] = total.astype(BF16)

    def expert_actions(s):
        part = functools.partial
        actions = []
        if s == 0:
            actions.append(lambda: [load.wait() for load in loads])
        actions += [part(select, s, 0), part(select, s, 1)]
        actions.append(lambda: pick_copy(s).start())
        actions.append(lambda: [copy.wait_send() for copy in ag_started[s]])
        actions.append(lambda: pick_copy(s).wait())
        actions += [part(ffn_up, s, c) for c in range(hidden_width // act_chunk)]
        actions += [part(ffn_down, s, c) for c in range(2 * half // chunk)]
        actions.append(lambda: back_copy(s).start())
        actions.append(lambda: back_copy(s).wait())
        actions += [
            part(partial_sums, s, grp, c) for grp in (0, 1) for c in range(2 * half // chunk)
        ]
        return actions

    rs_started = []

    def slot_ref(h, s, idx):
        return rbuf[h].at[s, pl.ds(idx * TOK, TOK), :]

    def rs_copy(h, s, idx, rows, to):
        return remote(
            gath[h].at[s, rows, pl.ds(0, half)], slot_ref(h, s, idx),
            rs_send.at[h, s, idx], rs_recv.at[h, s, idx], to,
        )

    def rs_actions(h, s):
        f, g = first[h], second[h]
        f_of = [shifted(f, off) for off in OFFSETS]

        def start(idx, rows, to):
            copy = rs_copy(h, s, idx, rows, to)
            copy.start()
            rs_started.append(copy)

        def wait(idx):
            rs_copy(h, s, idx, block(h, f, g, OWN), x_partner).wait_recv()

        def value(rows, slots):
            total = gath[h][s, rows, pl.ds(0, half)].astype(F32)
            for idx in slots:
                total += rbuf[h][s, pl.ds(idx * TOK, TOK), :].astype(F32)
            return total.astype(BF16)

        def store(rows, slots):
            gath[h][s, rows, pl.ds(0, half)] = value(rows, slots)

        def init_far(j):
            start(UP * 4 + j, block(h, f_of[j], shifted(g, 2), OWN), second_to(h, UP))
            start(DOWN * 4 + j, block(h, f_of[j], shifted(g, 2), OTHER), second_to(h, DOWN))

        def init_near(j):
            start(
                8 + UP * 8 + j * 2 + OTHER, block(h, f_of[j], shifted(g, 1), OTHER),
                second_to(h, UP),
            )
            start(
                8 + DOWN * 8 + j * 2 + OWN, block(h, f_of[j], shifted(g, 3), OWN),
                second_to(h, DOWN),
            )

        def add(j):
            up_rows = block(h, f_of[j], shifted(g, 1), OWN)
            down_rows = block(h, f_of[j], shifted(g, 3), OTHER)
            wait(UP * 4 + j)
            store(up_rows, [UP * 4 + j])
            wait(DOWN * 4 + j)
            store(down_rows, [DOWN * 4 + j])
            start(8 + UP * 8 + j * 2 + OWN, up_rows, second_to(h, UP))
            start(8 + DOWN * 8 + j * 2 + OTHER, down_rows, second_to(h, DOWN))

        def arrived(j, kind):
            slots = [8 + way * 8 + j * 2 + kind for way in (UP, DOWN)]
            for idx in slots:
                wait(idx)
            return slots

        def reduced(j, kind, extra, idx, way):
            slots = arrived(j, kind)
            for more in extra:
                wait(more)
            rows = block(h, f_of[j], g, kind)
            store(rows, slots + extra)
            start(idx, rows, first_to(h, way))

        def to_x():
            slots = arrived(0, OTHER) + [26 + UP * 2 + OTHER, 26 + DOWN * 2 + OTHER]
            for idx in slots[2:]:
                wait(idx)
            rows = block(h, f, g, OTHER)
            store(rows, slots)
            start(30, rows, x_partner)

        def finish():
            slots = arrived(0, OWN) + [26 + UP * 2 + OWN, 26 + DOWN * 2 + OWN, 30]
            for idx in slots[2:]:
                wait(idx)
            out_ref[pl.ds(s * TOK, TOK), pl.ds(h * half, half)] = value(
                block(h, f, g, OWN), slots
            )

        part = functools.partial
        order = (3, 2, 1, 0)
        head = [part(init_far, j) for j in order] + [part(init_near, j) for j in order]
        body = [part(add, j) for j in order]
        body += [
            part(reduced, 3, OWN, [], 24 + UP, UP),
            part(reduced, 3, OTHER, [], 24 + DOWN, DOWN),
            part(reduced, 2, OTHER, [], 26 + UP * 2 + OTHER, UP),
            part(reduced, 1, OWN, [], 26 + DOWN * 2 + OWN, DOWN),
            part(reduced, 2, OWN, [24 + UP], 26 + UP * 2 + OWN, UP),
            part(reduced, 1, OTHER, [24 + DOWN], 26 + DOWN * 2 + OTHER, DOWN),
            to_x,
        ]
        tail = [finish]
        return head, body, tail

    def run(actions):
        for action in actions:
            action()

    def blend(*lists):
        total = max(len(one) for one in lists)
        merged = []
        for index, one in enumerate(lists):
            for at, action in enumerate(one):
                merged.append(((at + 0.5) / len(one), index, at, action))
        merged.sort(key=lambda item: item[:3])
        return [item[3] for item in merged]

    ag = [both(ag_actions, s) for s in range(STEPS)]
    rs = [both(rs_actions, s) for s in range(STEPS)]
    ex = [expert_actions(s) for s in range(STEPS)]

    run(ag[0][0])
    for load in loads:
        load.start()
    run(ag[0][1])
    run(ag[1][0])
    run(ag[0][2])
    run(blend(ag[1][1], ex[0]))
    run(ag[2][0])
    run(rs[0][0])
    run(ag[1][2])
    run(blend(ag[2][1], ex[1], rs[0][1]))
    run(rs[1][0])
    run(ag[2][2])
    run(rs[0][2])
    run(blend(ex[2], rs[1][1]))
    run(rs[2][0])
    run(rs[1][2])
    run(rs[2][1])
    run(rs[2][2])
    for copy in rs_started:
        copy.wait_send()


def moe(experts, tok_a, tok_b, wgu, wd):
    rows, half = tok_b.shape
    depth, wide = wgu.shape
    hidden_width = wd.shape[0]
    vmem = pltpu.VMEM
    group_rows = GROUP * CAP
    own_rows = 2 * group_rows
    dma = pltpu.SemaphoreType.DMA
    return pl.pallas_call(
        moe_kernel,
        out_shape=jax.ShapeDtypeStruct((rows, 2 * half), BF16),
        in_specs=[
            pl.BlockSpec(memory_space=pltpu.SMEM),
            pl.BlockSpec(memory_space=vmem),
            pl.BlockSpec(memory_space=vmem),
            pl.BlockSpec(memory_space=pl.ANY),
            pl.BlockSpec(memory_space=pl.ANY),
        ],
        out_specs=pl.BlockSpec(memory_space=vmem),
        scratch_shapes=[
            vmem((STEPS, BLOCKS * TOK, half + META), BF16),
            vmem((STEPS, BLOCKS * TOK, half), BF16),
            vmem((STEPS, 31 * TOK, half), BF16),
            vmem((STEPS, 31 * TOK, half), BF16),
            vmem((depth, wide), BF16),
            vmem((hidden_width, depth), BF16),
            vmem((STEPS, 2 * own_rows, depth), BF16),
            vmem((2, own_rows, depth), BF16),
            vmem((own_rows, depth), BF16),
            vmem((2, own_rows, depth), BF16),
            vmem((STEPS, own_rows, depth), BF16),
            vmem((2 * own_rows, hidden_width), BF16),
            vmem((2, 256, 256), BF16),
            vmem((2, 256, 256), BF16),
            dma((2, STEPS, 31)),
            dma((2, STEPS, 31)),
            dma((2, STEPS, 31)),
            dma((2, STEPS, 31)),
            dma((2, STEPS)),
            dma((2, STEPS)),
            dma((2,)),
        ],
        compiler_params=pltpu.CompilerParams(
            collective_id=0, has_side_effects=True, vmem_limit_bytes=67043328
        ),
    )(experts, tok_a, tok_b, wgu, wd)


def on_device(hidden, expert_ids, gate_logits, w_gate_up, w_down, swap_step):
    devices = lax.axis_size("ep")
    my_index = lax.axis_index("ep")
    num_steps, tok_rows, model_dim = hidden.shape
    rows = num_steps * tok_rows
    pairs = [(source, source ^ 1) for source in range(devices)]
    other_down = lax.ppermute(w_down[0], "ep", pairs)

    exponent = jnp.exp(gate_logits)
    weights = exponent / jnp.sum(exponent, axis=-1, keepdims=True)
    high = lax.reduce_precision(weights, 8, 7)
    low = weights - high
    meta = jnp.concatenate([expert_ids.astype(F32), high, low], axis=-1).reshape(rows, -1)
    meta = jnp.pad(meta, ((0, 0), (0, META - meta.shape[1]))).astype(BF16)
    tokens = hidden.reshape(rows, model_dim)
    half = model_dim // 2
    experts = jnp.stack([my_index, my_index ^ 1]).astype(F32)
    mixed = moe(
        experts,
        jnp.concatenate([tokens[:, :half], meta], axis=1),
        tokens[:, half:],
        w_gate_up[0],
        w_down[0],
    )
    relocated = jnp.where(swap_step[my_index] < num_steps, other_down, w_down[0])
    return (mixed.reshape(hidden.shape), relocated[None])


def solution(mesh):
    in_specs = (
        P(None, ("dp", "ep"), None),
        P(None, ("dp", "ep"), None),
        P(None, ("dp", "ep"), None),
        P("ep", None, None),
        P("ep", None, None),
        P("dp"),
    )
    out_specs = (P(None, ("dp", "ep"), None), P(("dp", "ep"), None, None))
    return jax.shard_map(
        on_device, mesh=mesh, in_specs=in_specs, out_specs=out_specs, check_vma=False
    )
```

```python
import functools

import jax
import jax.numpy as jnp
from jax import lax
from jax.experimental import pallas as pl
from jax.experimental.pallas import tpu as pltpu
from jax.sharding import PartitionSpec as P

CAP = 5
STEPS = 3
TOK = 16
RING = 4
BLOCKS = 32
GROUP = 16
META = 128
OWN, OTHER = 0, 1
UP, DOWN = 0, 1
LAG = 2
OFFSETS = (0, 3, 1, 2)
BF16 = jnp.bfloat16
F32 = jnp.float32


def moe_kernel(
    expert_ref, tok_a, tokens_ref, wgu_hbm, wd_hbm, out_ref,
    gath_a, gath_b, rbuf_a, rbuf_b, wgu, wd, picked, pick_send, out_own, out_send, out_recv,
    act, weight_hi, weight_lo,
    ag_send, ag_recv, rs_send, rs_recv, pair_send, pair_recv, load_sem,
):
    half = tokens_ref.shape[1] // 2
    hidden_width = wd.shape[0]
    gath = (gath_a, gath_b)
    rbuf = (rbuf_a, rbuf_b)
    tok = (tok_a, tokens_ref.at[:, pl.ds(half, half)])
    me = lax.axis_index("ep")
    my_dp = lax.axis_index("dp")
    core = me % 2
    xh = (me // 2) % 2
    y = (me // 4) % RING
    z = me // 16

    def device(zz, yy, xx, dp):
        return {"ep": ((zz * RING + yy) * 2 + xx) * 2 + core, "dp": dp}

    x_partner = device(z, y, 1 - xh, 1 - my_dp)
    core_partner = {"ep": me + 1 - 2 * core, "dp": my_dp}
    first = (z, y)
    second = (y, z)

    def place(h, f, g):
        return (f, g) if h == 0 else (g, f)

    def block(h, f, g, kind):
        zz, yy = place(h, f, g)
        xx = xh if kind == OWN else 1 - xh
        start = ((zz * RING + yy) * 2 + xx) * TOK
        return pl.ds(pl.multiple_of(start, TOK), TOK)

    def shifted(value, amount):
        return (value + amount) % RING

    def first_to(h, way):
        f = shifted(first[h], 1 if way == UP else 3)
        zz, yy = place(h, f, second[h])
        return device(zz, yy, xh, my_dp)

    def second_to(h, way):
        g = shifted(second[h], 1 if way == UP else 3)
        zz, yy = place(h, first[h], g)
        return device(zz, yy, xh, my_dp)

    def remote(src, dst, send, recv, to):
        return pltpu.make_async_remote_copy(
            src_ref=src, dst_ref=dst, send_sem=send, recv_sem=recv,
            device_id=to, device_id_type=pl.DeviceIdType.MESH,
        )

    loads = (
        pltpu.make_async_copy(wgu_hbm, wgu, load_sem.at[0]),
        pltpu.make_async_copy(wd_hbm, wd, load_sem.at[1]),
    )

    barrier = pltpu.get_barrier_semaphore()
    friends = [x_partner, core_partner] + [
        to(0, way) for to in (first_to, second_to) for way in (UP, DOWN)
    ]
    for friend in friends:
        pl.semaphore_signal(
            barrier, inc=1, device_id=friend, device_id_type=pl.DeviceIdType.MESH
        )
    pl.semaphore_wait(barrier, len(friends))

    ag_started = {}

    def ag_copy(h, s, idx, rows, to, from_input=False):
        source = (
            tok[h].at[pl.ds(s * TOK, TOK), :] if from_input else gath[h].at[s, rows, :]
        )
        return remote(
            source, gath[h].at[s, rows, :], ag_send.at[h, s, idx], ag_recv.at[h, s, idx], to
        )

    def ag_start(h, s, idx, rows, to, from_input=False):
        copy = ag_copy(h, s, idx, rows, to, from_input)
        copy.start()
        ag_started.setdefault(s, []).append(copy)

    def ag_wait(h, s, idx, rows):
        ag_copy(h, s, idx, rows, x_partner).wait_recv()

    def ag_actions(h, s):
        f, g = first[h], second[h]
        f_of = [shifted(f, off) for off in OFFSETS]

        def spread(j, kind, from_input=False):
            for way in (UP, DOWN):
                ag_start(
                    h, s, 7 + way * 8 + j * 2 + kind, block(h, f_of[j], g, kind),
                    second_to(h, way), from_input,
                )

        def init():
            mine = block(h, f, g, OWN)
            ag_start(h, s, 0, mine, x_partner, True)
            for way in (UP, DOWN):
                ag_start(h, s, 1 + way * 2 + OWN, mine, first_to(h, way), True)
            gath[h][s, mine, :] = tok[h][pl.ds(s * TOK, TOK), :]

        def init2():
            spread(0, OWN, True)

        def a1():
            theirs = block(h, f, g, OTHER)
            ag_wait(h, s, 0, theirs)
            for way in (UP, DOWN):
                ag_start(h, s, 1 + way * 2 + OTHER, theirs, first_to(h, way))
            spread(0, OTHER)

        def near(way, kind):
            j = 1 if way == UP else 2
            rows = block(h, f_of[j], g, kind)
            ag_wait(h, s, 1 + way * 2 + kind, rows)
            if (way, kind) == (UP, OWN) or (way, kind) == (DOWN, OTHER):
                ag_start(h, s, 5 + way, rows, first_to(h, way))
            spread(j, kind)

        def far(way):
            kind = OWN if way == UP else OTHER
            ag_wait(h, s, 5 + way, block(h, f_of[3], g, kind))
            spread(3, kind)

        def forward(j, kind):
            way = UP if kind == OWN else DOWN
            rows = block(h, f_of[j], shifted(g, 3 if way == UP else 1), kind)
            ag_wait(h, s, 7 + way * 8 + j * 2 + kind, rows)
            ag_start(h, s, 23 + way * 4 + j, rows, second_to(h, way))

        def last(j):
            ag_wait(h, s, 7 + DOWN * 8 + j * 2 + OWN, block(h, f_of[j], shifted(g, 1), OWN))
            ag_wait(h, s, 7 + UP * 8 + j * 2 + OTHER, block(h, f_of[j], shifted(g, 3), OTHER))
            ag_wait(h, s, 23 + UP * 4 + j, block(h, f_of[j], shifted(g, 2), OWN))
            ag_wait(h, s, 23 + DOWN * 4 + j, block(h, f_of[j], shifted(g, 2), OTHER))

        part = functools.partial
        head = [init, init2]
        body = [
            a1, part(near, UP, OWN), part(near, DOWN, OWN), part(forward, 0, OWN),
            part(near, UP, OTHER), part(near, DOWN, OTHER), part(forward, 0, OTHER),
            part(far, UP), part(far, DOWN),
            part(forward, 1, OWN), part(forward, 2, OWN),
            part(forward, 1, OTHER), part(forward, 2, OTHER),
            part(forward, 3, OWN), part(forward, 3, OTHER),
        ]
        tail = [part(last, j) for j in (0, 1, 2, 3)]
        return head, body, tail

    def both(make, s):
        a, b = make(0, s), make(1, s)
        return [
            [act_ for pair in zip(pa, pb) for act_ in pair] for pa, pb in zip(a, b)
        ]

    chunk = min(512, half)
    act_chunk = min(256, hidden_width)

    def routing(s, grp):
        meta = gath_a[s, pl.ds(grp * 256, 256), pl.ds(half, META)].astype(F32)
        lane = lax.broadcasted_iota(jnp.int32, (256, META), 1)
        row = lax.broadcasted_iota(jnp.int32, (256, 256), 0)
        col = lax.broadcasted_iota(jnp.int32, (256, 256), 1)
        lower = jnp.where(
            (row > col) & (row // TOK == col // TOK), 1.0, 0.0
        ).astype(BF16)
        base = ((row // TOK) * CAP).astype(F32)
        colf = col.astype(F32)
        slot = jnp.zeros((256, 256), F32)
        hi = jnp.zeros((256, 256), F32)
        lo = jnp.zeros((256, 256), F32)
        shifted_hi = pltpu.roll(meta, META - 8, axis=1)
        shifted_lo = pltpu.roll(meta, META - 16, axis=1)
        for kind in (0, 1):
            expert = expert_ref[kind]
            match = (meta == expert) & (lane < 8)
            names = jnp.sum(jnp.where(match, 1.0, 0.0), axis=1, keepdims=True)
            w_hi = jnp.sum(jnp.where(match, shifted_hi, 0.0), axis=1, keepdims=True)
            w_lo = jnp.sum(jnp.where(match, shifted_lo, 0.0), axis=1, keepdims=True)
            rank = jnp.dot(
                lower, jnp.broadcast_to(names, (256, 256)).astype(BF16),
                preferred_element_type=F32,
            )
            target = base + rank + float(kind * GROUP * CAP)
            here = jnp.where((colf == target) & (names > 0.5), 1.0, 0.0)
            slot += here
            hi += here * w_hi
            lo += here * w_lo
        weight_hi[grp] = hi.astype(BF16)
        weight_lo[grp] = lo.astype(BF16)
        return slot.T.astype(BF16)[: 2 * GROUP * CAP, :]

    group_rows = GROUP * CAP
    own_rows = 2 * group_rows

    def select(s, grp):
        onehot = routing(s, grp)
        for h in (0, 1):
            for c in range(half // chunk):
                got = jnp.dot(
                    onehot,
                    gath[h][s, pl.ds(grp * 256, 256), pl.ds(c * chunk, chunk)],
                    preferred_element_type=F32,
                ).astype(BF16)
                at = pl.ds(h * half + c * chunk, chunk)
                picked[s, pl.ds(grp * group_rows, group_rows), at] = got[:group_rows]
                pick_send[s % 2, pl.ds(grp * group_rows, group_rows), at] = got[group_rows:]
            pick_copy(s, grp, h).start()

    def pick_copy(s, grp, h):
        at = pl.ds(h * half, half)
        return remote(
            pick_send.at[s % 2, pl.ds(grp * group_rows, group_rows), at],
            picked.at[s, pl.ds(own_rows + grp * group_rows, group_rows), at],
            pair_send.at[0, s, grp * 2 + h], pair_recv.at[0, s, grp * 2 + h], core_partner,
        )

    def back_copy(s, c):
        at = pl.ds(c * chunk, chunk)
        return remote(
            out_send.at[s % 2, :, at], out_recv.at[s, :, at],
            pair_send.at[1, s, c], pair_recv.at[1, s, c], core_partner,
        )

    def ffn_up(s, c):
        rows = picked[s]
        gate = jnp.dot(rows, wgu[:, pl.ds(c * act_chunk, act_chunk)], preferred_element_type=F32)
        up = jnp.dot(
            rows, wgu[:, pl.ds(hidden_width + c * act_chunk, act_chunk)],
            preferred_element_type=F32,
        )
        act[:, pl.ds(c * act_chunk, act_chunk)] = (
            gate / (1.0 + jnp.exp(-gate)) * up
        ).astype(BF16)

    def ffn_down(s, c):
        at = pl.ds(c * chunk, chunk)
        got = jnp.dot(act[...], wd[:, at], preferred_element_type=F32).astype(BF16)
        out_own[:, at] = got[:own_rows]
        out_send[s % 2, :, at] = got[own_rows:]
        back_copy(s, c).start()

    def partial_sums(s, grp, c):
        rows = pl.ds(grp * group_rows, group_rows)
        h, offset = divmod(c * chunk, half)
        at = pl.ds(c * chunk, chunk)
        outs = jnp.concatenate([out_own[rows, at], out_recv[s, rows, at]], axis=0)
        total = jnp.dot(
            weight_hi[grp, :, : 2 * group_rows], outs, preferred_element_type=F32
        ) + jnp.dot(weight_lo[grp, :, : 2 * group_rows], outs, preferred_element_type=F32)
        gath[h][s, pl.ds(grp * 256, 256), pl.ds(offset, chunk)] = total.astype(BF16)

    def expert_actions(s):
        part = functools.partial
        chunks = 2 * half // chunk
        lag = min(LAG, chunks)
        actions = [part(select, s, 0), part(select, s, 1)]
        if s == 0:
            actions.append(lambda: [load.wait() for load in loads])
        actions.append(lambda: [copy.wait_send() for copy in ag_started[s]])
        actions.append(
            lambda: [pick_copy(s, grp, h).wait() for grp in (0, 1) for h in (0, 1)]
        )
        actions += [part(ffn_up, s, c) for c in range(hidden_width // act_chunk)]
        for c in range(chunks + lag):
            if c < chunks:
                actions.append(part(ffn_down, s, c))
            if c >= lag:
                actions.append(lambda c=c: back_copy(s, c - lag).wait())
                actions += [part(partial_sums, s, grp, c - lag) for grp in (0, 1)]
                for h in (0, 1):
                    if (c - lag + 1) * chunk == (h + 1) * half:
                        actions.append(part(run, rs_parts[s][h][0]))
        return actions

    rs_started = []

    def slot_ref(h, s, idx):
        return rbuf[h].at[s, pl.ds(idx * TOK, TOK), :]

    def rs_copy(h, s, idx, rows, to):
        return remote(
            gath[h].at[s, rows, pl.ds(0, half)], slot_ref(h, s, idx),
            rs_send.at[h, s, idx], rs_recv.at[h, s, idx], to,
        )

    def rs_actions(h, s):
        f, g = first[h], second[h]
        f_of = [shifted(f, off) for off in OFFSETS]

        def start(idx, rows, to):
            copy = rs_copy(h, s, idx, rows, to)
            copy.start()
            rs_started.append(copy)

        def wait(idx):
            rs_copy(h, s, idx, block(h, f, g, OWN), x_partner).wait_recv()

        def value(rows, slots):
            total = gath[h][s, rows, pl.ds(0, half)].astype(F32)
            for idx in slots:
                total += rbuf[h][s, pl.ds(idx * TOK, TOK), :].astype(F32)
            return total.astype(BF16)

        def store(rows, slots):
            gath[h][s, rows, pl.ds(0, half)] = value(rows, slots)

        def init_far(j):
            start(UP * 4 + j, block(h, f_of[j], shifted(g, 2), OWN), second_to(h, UP))
            start(DOWN * 4 + j, block(h, f_of[j], shifted(g, 2), OTHER), second_to(h, DOWN))

        def init_near(j):
            start(
                8 + UP * 8 + j * 2 + OTHER, block(h, f_of[j], shifted(g, 1), OTHER),
                second_to(h, UP),
            )
            start(
                8 + DOWN * 8 + j * 2 + OWN, block(h, f_of[j], shifted(g, 3), OWN),
                second_to(h, DOWN),
            )

        def add(j):
            up_rows = block(h, f_of[j], shifted(g, 1), OWN)
            down_rows = block(h, f_of[j], shifted(g, 3), OTHER)
            wait(UP * 4 + j)
            store(up_rows, [UP * 4 + j])
            wait(DOWN * 4 + j)
            store(down_rows, [DOWN * 4 + j])
            start(8 + UP * 8 + j * 2 + OWN, up_rows, second_to(h, UP))
            start(8 + DOWN * 8 + j * 2 + OTHER, down_rows, second_to(h, DOWN))

        def arrived(j, kind):
            slots = [8 + way * 8 + j * 2 + kind for way in (UP, DOWN)]
            for idx in slots:
                wait(idx)
            return slots

        def reduced(j, kind, extra, idx, way):
            slots = arrived(j, kind)
            for more in extra:
                wait(more)
            rows = block(h, f_of[j], g, kind)
            store(rows, slots + extra)
            start(idx, rows, first_to(h, way))

        def to_x():
            slots = arrived(0, OTHER) + [26 + UP * 2 + OTHER, 26 + DOWN * 2 + OTHER]
            for idx in slots[2:]:
                wait(idx)
            rows = block(h, f, g, OTHER)
            store(rows, slots)
            start(30, rows, x_partner)

        def finish():
            slots = arrived(0, OWN) + [26 + UP * 2 + OWN, 26 + DOWN * 2 + OWN, 30]
            for idx in slots[2:]:
                wait(idx)
            out_ref[pl.ds(s * TOK, TOK), pl.ds(h * half, half)] = value(
                block(h, f, g, OWN), slots
            )

        part = functools.partial
        order = (3, 2, 1, 0)
        head = [part(init_far, j) for j in order] + [part(init_near, j) for j in order]
        body = [part(add, j) for j in order]
        body += [
            part(reduced, 3, OWN, [], 24 + UP, UP),
            part(reduced, 3, OTHER, [], 24 + DOWN, DOWN),
            part(reduced, 2, OTHER, [], 26 + UP * 2 + OTHER, UP),
            part(reduced, 1, OWN, [], 26 + DOWN * 2 + OWN, DOWN),
            part(reduced, 2, OWN, [24 + UP], 26 + UP * 2 + OWN, UP),
            part(reduced, 1, OTHER, [24 + DOWN], 26 + DOWN * 2 + OTHER, DOWN),
            to_x,
        ]
        tail = [finish]
        return head, body, tail

    def run(actions):
        for action in actions:
            action()

    def blend(*lists):
        total = max(len(one) for one in lists)
        merged = []
        for index, one in enumerate(lists):
            for at, action in enumerate(one):
                merged.append(((at + 0.5) / len(one), index, at, action))
        merged.sort(key=lambda item: item[:3])
        return [item[3] for item in merged]

    ag = [both(ag_actions, s) for s in range(STEPS)]
    rs_parts = [[rs_actions(h, s) for h in (0, 1)] for s in range(STEPS)]
    rs = [
        [[act_ for pair in zip(pa, pb) for act_ in pair] for pa, pb in zip(*parts)]
        for parts in rs_parts
    ]
    ex = [expert_actions(s) for s in range(STEPS)]

    run(ag[0][0])
    for load in loads:
        load.start()
    run(ag[0][1])
    run(ag[1][0])
    run(ag[0][2])
    run(blend(ag[1][1] + ag[2][0], ex[0]))
    run(ag[1][2])
    run(blend(ag[2][1], ex[1], rs[0][1]))
    run(ag[2][2])
    run(rs[0][2])
    run(blend(ex[2], rs[1][1]))
    run(rs[1][2])
    run(rs[2][1])
    run(rs[2][2])
    for copy in rs_started:
        copy.wait_send()


def moe(experts, tok_a, tokens, wgu, wd):
    rows, half = tokens.shape[0], tokens.shape[1] // 2
    depth, wide = wgu.shape
    hidden_width = wd.shape[0]
    vmem = pltpu.VMEM
    group_rows = GROUP * CAP
    own_rows = 2 * group_rows
    dma = pltpu.SemaphoreType.DMA
    return pl.pallas_call(
        moe_kernel,
        out_shape=jax.ShapeDtypeStruct((rows, 2 * half), BF16),
        in_specs=[
            pl.BlockSpec(memory_space=pltpu.SMEM),
            pl.BlockSpec(memory_space=vmem),
            pl.BlockSpec(memory_space=vmem),
            pl.BlockSpec(memory_space=pl.ANY),
            pl.BlockSpec(memory_space=pl.ANY),
        ],
        out_specs=pl.BlockSpec(memory_space=vmem),
        scratch_shapes=[
            vmem((STEPS, BLOCKS * TOK, half + META), BF16),
            vmem((STEPS, BLOCKS * TOK, half), BF16),
            vmem((STEPS, 31 * TOK, half), BF16),
            vmem((STEPS, 31 * TOK, half), BF16),
            vmem((depth, wide), BF16),
            vmem((hidden_width, depth), BF16),
            vmem((STEPS, 2 * own_rows, depth), BF16),
            vmem((2, own_rows, depth), BF16),
            vmem((own_rows, depth), BF16),
            vmem((2, own_rows, depth), BF16),
            vmem((STEPS, own_rows, depth), BF16),
            vmem((2 * own_rows, hidden_width), BF16),
            vmem((2, 256, 256), BF16),
            vmem((2, 256, 256), BF16),
            dma((2, STEPS, 31)),
            dma((2, STEPS, 31)),
            dma((2, STEPS, 31)),
            dma((2, STEPS, 31)),
            dma((2, STEPS, 8)),
            dma((2, STEPS, 8)),
            dma((2,)),
        ],
        compiler_params=pltpu.CompilerParams(
            collective_id=0, has_side_effects=True, vmem_limit_bytes=67043328
        ),
    )(experts, tok_a, tokens, wgu, wd)


def on_device(hidden, expert_ids, gate_logits, w_gate_up, w_down, swap_step):
    devices = lax.axis_size("ep")
    my_index = lax.axis_index("ep")
    num_steps, tok_rows, model_dim = hidden.shape
    rows = num_steps * tok_rows
    pairs = [(source, source ^ 1) for source in range(devices)]
    other_down = lax.ppermute(w_down[0], "ep", pairs)

    exponent = jnp.exp(gate_logits)
    weights = exponent / jnp.sum(exponent, axis=-1, keepdims=True)
    high = lax.reduce_precision(weights, 8, 7)
    low = weights - high
    meta = jnp.concatenate([expert_ids.astype(F32), high, low], axis=-1).reshape(rows, -1)
    meta = jnp.pad(meta, ((0, 0), (0, META - meta.shape[1]))).astype(BF16)
    tokens = hidden.reshape(rows, model_dim)
    half = model_dim // 2
    experts = jnp.stack([my_index, my_index ^ 1]).astype(F32)
    mixed = moe(
        experts,
        jnp.concatenate([tokens[:, :half], meta], axis=1),
        tokens,
        w_gate_up[0],
        w_down[0],
    )
    relocated = jnp.where(swap_step[my_index] < num_steps, other_down, w_down[0])
    return (mixed.reshape(hidden.shape), relocated[None])


def solution(mesh):
    in_specs = (
        P(None, ("dp", "ep"), None),
        P(None, ("dp", "ep"), None),
        P(None, ("dp", "ep"), None),
        P("ep", None, None),
        P("ep", None, None),
        P("dp"),
    )
    out_specs = (P(None, ("dp", "ep"), None), P(("dp", "ep"), None, None))
    return jax.shard_map(
        on_device, mesh=mesh, in_specs=in_specs, out_specs=out_specs, check_vma=False
    )
```

```python
import functools

import jax
import jax.numpy as jnp
from jax import lax
from jax.experimental import pallas as pl
from jax.experimental.pallas import tpu as pltpu
from jax.sharding import PartitionSpec as P

CAP = 5
STEPS = 3
TOK = 16
RING = 4
BLOCKS = 32
GROUP = 16
META = 128
OWN, OTHER = 0, 1
UP, DOWN = 0, 1
LAG = 4
OFFSETS = (0, 3, 1, 2)
BF16 = jnp.bfloat16
F32 = jnp.float32


def moe_kernel(
    expert_ref, tok_a, tokens_ref, wgu_hbm, wd_hbm, out_ref,
    gath_a, gath_b, rbuf_a, rbuf_b, wgu, wd, picked, pick_send, out_own, out_send, out_recv,
    act, weight_hi, weight_lo,
    ag_send, ag_recv, rs_send, rs_recv, pair_send, pair_recv, load_sem,
):
    half = tokens_ref.shape[1] // 2
    hidden_width = wd.shape[0]
    gath = (gath_a, gath_b)
    rbuf = (rbuf_a, rbuf_b)
    tok = (tok_a, tokens_ref.at[:, pl.ds(half, half)])
    me = lax.axis_index("ep")
    my_dp = lax.axis_index("dp")
    core = me % 2
    xh = (me // 2) % 2
    y = (me // 4) % RING
    z = me // 16

    def device(zz, yy, xx, dp):
        return {"ep": ((zz * RING + yy) * 2 + xx) * 2 + core, "dp": dp}

    x_partner = device(z, y, 1 - xh, 1 - my_dp)
    core_partner = {"ep": me + 1 - 2 * core, "dp": my_dp}
    first = (z, y)
    second = (y, z)

    def place(h, f, g):
        return (f, g) if h == 0 else (g, f)

    def block(h, f, g, kind):
        zz, yy = place(h, f, g)
        xx = xh if kind == OWN else 1 - xh
        start = ((zz * RING + yy) * 2 + xx) * TOK
        return pl.ds(pl.multiple_of(start, TOK), TOK)

    def shifted(value, amount):
        return (value + amount) % RING

    def first_to(h, way):
        f = shifted(first[h], 1 if way == UP else 3)
        zz, yy = place(h, f, second[h])
        return device(zz, yy, xh, my_dp)

    def second_to(h, way):
        g = shifted(second[h], 1 if way == UP else 3)
        zz, yy = place(h, first[h], g)
        return device(zz, yy, xh, my_dp)

    def remote(src, dst, send, recv, to):
        return pltpu.make_async_remote_copy(
            src_ref=src, dst_ref=dst, send_sem=send, recv_sem=recv,
            device_id=to, device_id_type=pl.DeviceIdType.MESH,
        )

    loads = (
        pltpu.make_async_copy(wgu_hbm, wgu, load_sem.at[0]),
        pltpu.make_async_copy(wd_hbm, wd, load_sem.at[1]),
    )

    barrier = pltpu.get_barrier_semaphore()
    friends = [x_partner, core_partner] + [
        to(0, way) for to in (first_to, second_to) for way in (UP, DOWN)
    ]
    for friend in friends:
        pl.semaphore_signal(
            barrier, inc=1, device_id=friend, device_id_type=pl.DeviceIdType.MESH
        )
    pl.semaphore_wait(barrier, len(friends))

    ag_started = {}

    def ag_copy(h, s, idx, rows, to, from_input=False):
        source = (
            tok[h].at[pl.ds(s * TOK, TOK), :] if from_input else gath[h].at[s, rows, :]
        )
        return remote(
            source, gath[h].at[s, rows, :], ag_send.at[h, s, idx], ag_recv.at[h, s, idx], to
        )

    def ag_start(h, s, idx, rows, to, from_input=False):
        copy = ag_copy(h, s, idx, rows, to, from_input)
        copy.start()
        ag_started.setdefault(s, []).append(copy)

    def ag_wait(h, s, idx, rows):
        ag_copy(h, s, idx, rows, x_partner).wait_recv()

    def ag_actions(h, s):
        f, g = first[h], second[h]
        f_of = [shifted(f, off) for off in OFFSETS]

        def spread(j, kind, from_input=False):
            for way in (UP, DOWN):
                ag_start(
                    h, s, 7 + way * 8 + j * 2 + kind, block(h, f_of[j], g, kind),
                    second_to(h, way), from_input,
                )

        def init():
            mine = block(h, f, g, OWN)
            ag_start(h, s, 0, mine, x_partner, True)
            for way in (UP, DOWN):
                ag_start(h, s, 1 + way * 2 + OWN, mine, first_to(h, way), True)
            gath[h][s, mine, :] = tok[h][pl.ds(s * TOK, TOK), :]

        def init2():
            spread(0, OWN, True)

        def a1():
            theirs = block(h, f, g, OTHER)
            ag_wait(h, s, 0, theirs)
            for way in (UP, DOWN):
                ag_start(h, s, 1 + way * 2 + OTHER, theirs, first_to(h, way))
            spread(0, OTHER)

        def near(way, kind):
            j = 1 if way == UP else 2
            rows = block(h, f_of[j], g, kind)
            ag_wait(h, s, 1 + way * 2 + kind, rows)
            if (way, kind) == (UP, OWN) or (way, kind) == (DOWN, OTHER):
                ag_start(h, s, 5 + way, rows, first_to(h, way))
            spread(j, kind)

        def far(way):
            kind = OWN if way == UP else OTHER
            ag_wait(h, s, 5 + way, block(h, f_of[3], g, kind))
            spread(3, kind)

        def forward(j, kind):
            way = UP if kind == OWN else DOWN
            rows = block(h, f_of[j], shifted(g, 3 if way == UP else 1), kind)
            ag_wait(h, s, 7 + way * 8 + j * 2 + kind, rows)
            ag_start(h, s, 23 + way * 4 + j, rows, second_to(h, way))

        def last(j):
            ag_wait(h, s, 7 + DOWN * 8 + j * 2 + OWN, block(h, f_of[j], shifted(g, 1), OWN))
            ag_wait(h, s, 7 + UP * 8 + j * 2 + OTHER, block(h, f_of[j], shifted(g, 3), OTHER))
            ag_wait(h, s, 23 + UP * 4 + j, block(h, f_of[j], shifted(g, 2), OWN))
            ag_wait(h, s, 23 + DOWN * 4 + j, block(h, f_of[j], shifted(g, 2), OTHER))

        part = functools.partial
        head = [init, init2]
        body = [
            a1, part(near, UP, OWN), part(near, DOWN, OWN), part(forward, 0, OWN),
            part(near, UP, OTHER), part(near, DOWN, OTHER), part(forward, 0, OTHER),
            part(far, UP), part(far, DOWN),
            part(forward, 1, OWN), part(forward, 2, OWN),
            part(forward, 1, OTHER), part(forward, 2, OTHER),
            part(forward, 3, OWN), part(forward, 3, OTHER),
        ]
        tail = [part(last, j) for j in (0, 1, 2, 3)]
        return head, body, tail

    def both(make, s):
        a, b = make(0, s), make(1, s)
        return [
            [act_ for pair in zip(pa, pb) for act_ in pair] for pa, pb in zip(a, b)
        ]

    chunk = min(512, half)
    act_chunk = min(256, hidden_width)

    def routing(s, grp):
        meta = gath_a[s, pl.ds(grp * 256, 256), pl.ds(half, META)].astype(F32)
        lane = lax.broadcasted_iota(jnp.int32, (256, META), 1)
        row = lax.broadcasted_iota(jnp.int32, (256, 256), 0)
        col = lax.broadcasted_iota(jnp.int32, (256, 256), 1)
        lower = jnp.where(
            (row > col) & (row // TOK == col // TOK), 1.0, 0.0
        ).astype(BF16)
        base = ((row // TOK) * CAP).astype(F32)
        colf = col.astype(F32)
        slot = jnp.zeros((256, 256), F32)
        hi = jnp.zeros((256, 256), F32)
        lo = jnp.zeros((256, 256), F32)
        shifted_hi = pltpu.roll(meta, META - 8, axis=1)
        shifted_lo = pltpu.roll(meta, META - 16, axis=1)
        for kind in (0, 1):
            expert = expert_ref[kind]
            match = (meta == expert) & (lane < 8)
            names = jnp.sum(jnp.where(match, 1.0, 0.0), axis=1, keepdims=True)
            w_hi = jnp.sum(jnp.where(match, shifted_hi, 0.0), axis=1, keepdims=True)
            w_lo = jnp.sum(jnp.where(match, shifted_lo, 0.0), axis=1, keepdims=True)
            rank = jnp.dot(
                lower, jnp.broadcast_to(names, (256, 256)).astype(BF16),
                preferred_element_type=F32,
            )
            target = base + rank + float(kind * GROUP * CAP)
            here = jnp.where((colf == target) & (names > 0.5), 1.0, 0.0)
            slot += here
            hi += here * w_hi
            lo += here * w_lo
        weight_hi[grp] = hi.astype(BF16)
        weight_lo[grp] = lo.astype(BF16)
        return slot.T.astype(BF16)[: 2 * GROUP * CAP, :]

    group_rows = GROUP * CAP
    own_rows = 2 * group_rows

    def select(s, grp):
        onehot = routing(s, grp)
        for h in (0, 1):
            for c in range(half // chunk):
                got = jnp.dot(
                    onehot,
                    gath[h][s, pl.ds(grp * 256, 256), pl.ds(c * chunk, chunk)],
                    preferred_element_type=F32,
                ).astype(BF16)
                at = pl.ds(h * half + c * chunk, chunk)
                picked[s, pl.ds(grp * group_rows, group_rows), at] = got[:group_rows]
                pick_send[s % 2, pl.ds(grp * group_rows, group_rows), at] = got[group_rows:]
            pick_copy(s, grp, h).start()

    def pick_copy(s, grp, h):
        at = pl.ds(h * half, half)
        return remote(
            pick_send.at[s % 2, pl.ds(grp * group_rows, group_rows), at],
            picked.at[s, pl.ds(own_rows + grp * group_rows, group_rows), at],
            pair_send.at[0, s, grp * 2 + h], pair_recv.at[0, s, grp * 2 + h], core_partner,
        )

    def back_copy(s, c):
        at = pl.ds(c * chunk, chunk)
        return remote(
            out_send.at[s % 2, :, at], out_recv.at[s, :, at],
            pair_send.at[1, s, c], pair_recv.at[1, s, c], core_partner,
        )

    def ffn_up(s, c):
        rows = picked[s]
        gate = jnp.dot(rows, wgu[:, pl.ds(c * act_chunk, act_chunk)], preferred_element_type=F32)
        up = jnp.dot(
            rows, wgu[:, pl.ds(hidden_width + c * act_chunk, act_chunk)],
            preferred_element_type=F32,
        )
        act[:, pl.ds(c * act_chunk, act_chunk)] = (
            gate / (1.0 + jnp.exp(-gate)) * up
        ).astype(BF16)

    def ffn_down(s, c):
        at = pl.ds(c * chunk, chunk)
        got = jnp.dot(act[...], wd[:, at], preferred_element_type=F32).astype(BF16)
        out_own[:, at] = got[:own_rows]
        out_send[s % 2, :, at] = got[own_rows:]
        back_copy(s, c).start()

    def partial_sums(s, grp, c):
        rows = pl.ds(grp * group_rows, group_rows)
        h, offset = divmod(c * chunk, half)
        at = pl.ds(c * chunk, chunk)
        outs = jnp.concatenate([out_own[rows, at], out_recv[s, rows, at]], axis=0)
        total = jnp.dot(
            weight_hi[grp, :, : 2 * group_rows], outs, preferred_element_type=F32
        ) + jnp.dot(weight_lo[grp, :, : 2 * group_rows], outs, preferred_element_type=F32)
        gath[h][s, pl.ds(grp * 256, 256), pl.ds(offset, chunk)] = total.astype(BF16)

    def expert_actions(s):
        part = functools.partial
        chunks = 2 * half // chunk
        lag = min(LAG, chunks)
        actions = [(1.5, part(select, s, 0)), (1.5, part(select, s, 1))]

        def add(weight, action):
            actions.append((weight, action))

        if s == 0:
            add(0, lambda: [load.wait() for load in loads])
        add(0, lambda: [copy.wait_send() for copy in ag_started[s]])
        add(0.5, lambda: [pick_copy(s, grp, h).wait() for grp in (0, 1) for h in (0, 1)])
        for c in range(hidden_width // act_chunk):
            add(2.0, part(ffn_up, s, c))
        for c in range(chunks + lag):
            if c < chunks:
                add(0.4, part(ffn_down, s, c))
            if c >= lag:
                add(0.1, lambda c=c: back_copy(s, c - lag).wait())
                for grp in (0, 1):
                    add(0.3, part(partial_sums, s, grp, c - lag))
        return actions

    rs_started = []

    def slot_ref(h, s, idx):
        return rbuf[h].at[s, pl.ds(idx * TOK, TOK), :]

    def rs_copy(h, s, idx, rows, to):
        return remote(
            gath[h].at[s, rows, pl.ds(0, half)], slot_ref(h, s, idx),
            rs_send.at[h, s, idx], rs_recv.at[h, s, idx], to,
        )

    def rs_actions(h, s):
        f, g = first[h], second[h]
        f_of = [shifted(f, off) for off in OFFSETS]

        def start(idx, rows, to):
            copy = rs_copy(h, s, idx, rows, to)
            copy.start()
            rs_started.append(copy)

        def wait(idx):
            rs_copy(h, s, idx, block(h, f, g, OWN), x_partner).wait_recv()

        def value(rows, slots):
            total = gath[h][s, rows, pl.ds(0, half)].astype(F32)
            for idx in slots:
                total += rbuf[h][s, pl.ds(idx * TOK, TOK), :].astype(F32)
            return total.astype(BF16)

        def store(rows, slots):
            gath[h][s, rows, pl.ds(0, half)] = value(rows, slots)

        def init_far(j):
            start(UP * 4 + j, block(h, f_of[j], shifted(g, 2), OWN), second_to(h, UP))
            start(DOWN * 4 + j, block(h, f_of[j], shifted(g, 2), OTHER), second_to(h, DOWN))

        def init_near(j):
            start(
                8 + UP * 8 + j * 2 + OTHER, block(h, f_of[j], shifted(g, 1), OTHER),
                second_to(h, UP),
            )
            start(
                8 + DOWN * 8 + j * 2 + OWN, block(h, f_of[j], shifted(g, 3), OWN),
                second_to(h, DOWN),
            )

        def add(j):
            up_rows = block(h, f_of[j], shifted(g, 1), OWN)
            down_rows = block(h, f_of[j], shifted(g, 3), OTHER)
            wait(UP * 4 + j)
            store(up_rows, [UP * 4 + j])
            wait(DOWN * 4 + j)
            store(down_rows, [DOWN * 4 + j])
            start(8 + UP * 8 + j * 2 + OWN, up_rows, second_to(h, UP))
            start(8 + DOWN * 8 + j * 2 + OTHER, down_rows, second_to(h, DOWN))

        def arrived(j, kind):
            slots = [8 + way * 8 + j * 2 + kind for way in (UP, DOWN)]
            for idx in slots:
                wait(idx)
            return slots

        def reduced(j, kind, extra, idx, way):
            slots = arrived(j, kind)
            for more in extra:
                wait(more)
            rows = block(h, f_of[j], g, kind)
            store(rows, slots + extra)
            start(idx, rows, first_to(h, way))

        def to_x():
            slots = arrived(0, OTHER) + [26 + UP * 2 + OTHER, 26 + DOWN * 2 + OTHER]
            for idx in slots[2:]:
                wait(idx)
            rows = block(h, f, g, OTHER)
            store(rows, slots)
            start(30, rows, x_partner)

        def finish():
            slots = arrived(0, OWN) + [26 + UP * 2 + OWN, 26 + DOWN * 2 + OWN, 30]
            for idx in slots[2:]:
                wait(idx)
            out_ref[pl.ds(s * TOK, TOK), pl.ds(h * half, half)] = value(
                block(h, f, g, OWN), slots
            )

        part = functools.partial
        order = (3, 2, 1, 0)
        head = [part(init_far, j) for j in order] + [part(init_near, j) for j in order]
        body = [part(add, j) for j in order]
        body += [
            part(reduced, 3, OWN, [], 24 + UP, UP),
            part(reduced, 3, OTHER, [], 24 + DOWN, DOWN),
            part(reduced, 2, OTHER, [], 26 + UP * 2 + OTHER, UP),
            part(reduced, 1, OWN, [], 26 + DOWN * 2 + OWN, DOWN),
            part(reduced, 2, OWN, [24 + UP], 26 + UP * 2 + OWN, UP),
            part(reduced, 1, OTHER, [24 + DOWN], 26 + DOWN * 2 + OTHER, DOWN),
            to_x,
        ]
        tail = [finish]
        return head, body, tail

    def run(actions):
        for action in actions:
            action()

    def blend(*lists):
        merged = []
        for index, one in enumerate(lists):
            pairs = [item if isinstance(item, tuple) else (1, item) for item in one]
            total, before = sum(weight for weight, _ in pairs), 0
            for at, (weight, action) in enumerate(pairs):
                merged.append(((before + 0.5 * weight) / total, index, at, action))
                before += weight
        merged.sort(key=lambda item: item[:3])
        return [item[3] for item in merged]

    ag = [both(ag_actions, s) for s in range(STEPS)]
    rs = [both(rs_actions, s) for s in range(STEPS)]
    ex = [expert_actions(s) for s in range(STEPS)]

    run(ag[0][0])
    for load in loads:
        load.start()
    run(ag[0][1])
    run(ag[1][0])
    run(ag[0][2])
    run(blend(ag[1][1], ex[0]))
    run(ag[2][0])
    run(rs[0][0])
    run(ag[1][2])
    run(blend(ag[2][1], ex[1], rs[0][1]))
    run(rs[1][0])
    run(ag[2][2])
    run(rs[0][2])
    run(blend(ex[2], rs[1][1]))
    run(rs[2][0])
    run(rs[1][2])
    run(rs[2][1])
    run(rs[2][2])
    for copy in rs_started:
        copy.wait_send()


def moe(experts, tok_a, tokens, wgu, wd):
    rows, half = tokens.shape[0], tokens.shape[1] // 2
    depth, wide = wgu.shape
    hidden_width = wd.shape[0]
    vmem = pltpu.VMEM
    group_rows = GROUP * CAP
    own_rows = 2 * group_rows
    dma = pltpu.SemaphoreType.DMA
    return pl.pallas_call(
        moe_kernel,
        out_shape=jax.ShapeDtypeStruct((rows, 2 * half), BF16),
        in_specs=[
            pl.BlockSpec(memory_space=pltpu.SMEM),
            pl.BlockSpec(memory_space=vmem),
            pl.BlockSpec(memory_space=vmem),
            pl.BlockSpec(memory_space=pl.ANY),
            pl.BlockSpec(memory_space=pl.ANY),
        ],
        out_specs=pl.BlockSpec(memory_space=vmem),
        scratch_shapes=[
            vmem((STEPS, BLOCKS * TOK, half + META), BF16),
            vmem((STEPS, BLOCKS * TOK, half), BF16),
            vmem((STEPS, 31 * TOK, half), BF16),
            vmem((STEPS, 31 * TOK, half), BF16),
            vmem((depth, wide), BF16),
            vmem((hidden_width, depth), BF16),
            vmem((STEPS, 2 * own_rows, depth), BF16),
            vmem((2, own_rows, depth), BF16),
            vmem((own_rows, depth), BF16),
            vmem((2, own_rows, depth), BF16),
            vmem((STEPS, own_rows, depth), BF16),
            vmem((2 * own_rows, hidden_width), BF16),
            vmem((2, 256, 256), BF16),
            vmem((2, 256, 256), BF16),
            dma((2, STEPS, 31)),
            dma((2, STEPS, 31)),
            dma((2, STEPS, 31)),
            dma((2, STEPS, 31)),
            dma((2, STEPS, 8)),
            dma((2, STEPS, 8)),
            dma((2,)),
        ],
        compiler_params=pltpu.CompilerParams(
            collective_id=0, has_side_effects=True, vmem_limit_bytes=67043328
        ),
    )(experts, tok_a, tokens, wgu, wd)


PIECES = 6


def relocate_kernel(swap_ref, own, other, out, held, in_sem, out_sem):
    depth = held.shape[0] // PIECES
    moved = swap_ref[lax.axis_index("ep")] < STEPS
    parts = [pl.ds(i * depth, depth) for i in range(PIECES)]

    def load(source, i):
        return pltpu.make_async_copy(
            source.at[parts[i], :], held.at[parts[i], :], in_sem.at[i]
        )

    for source, wanted in ((other, moved), (own, jnp.logical_not(moved))):

        @pl.when(wanted)
        def _():
            for i in range(PIECES):
                load(source, i).start()

    stores = []
    for i in range(PIECES):
        load(own, i).wait()
        stores.append(
            pltpu.make_async_copy(held.at[parts[i], :], out.at[parts[i], :], out_sem.at[i])
        )
        stores[-1].start()
    for store in stores:
        store.wait()


def relocate(swap_step, own, other):
    return pl.pallas_call(
        relocate_kernel,
        out_shape=jax.ShapeDtypeStruct(own.shape, own.dtype),
        in_specs=[pl.BlockSpec(memory_space=pltpu.SMEM)]
        + [pl.BlockSpec(memory_space=pl.ANY)] * 2,
        out_specs=pl.BlockSpec(memory_space=pl.ANY),
        scratch_shapes=[
            pltpu.VMEM(own.shape, own.dtype),
            pltpu.SemaphoreType.DMA((PIECES,)),
            pltpu.SemaphoreType.DMA((PIECES,)),
        ],
        cost_estimate=pl.CostEstimate(
            flops=0, bytes_accessed=4 * own.size, transcendentals=0
        ),
    )(swap_step, own, other)


def on_device(hidden, expert_ids, gate_logits, w_gate_up, w_down, swap_step):
    devices = lax.axis_size("ep")
    my_index = lax.axis_index("ep")
    num_steps, tok_rows, model_dim = hidden.shape
    rows = num_steps * tok_rows
    pairs = [(source, source ^ 1) for source in range(devices)]
    other_down = lax.ppermute(w_down[0], "ep", pairs)

    exponent = jnp.exp(gate_logits)
    weights = exponent / jnp.sum(exponent, axis=-1, keepdims=True)
    high = lax.reduce_precision(weights, 8, 7)
    low = weights - high
    meta = jnp.concatenate([expert_ids.astype(F32), high, low], axis=-1).reshape(rows, -1)
    meta = jnp.pad(meta, ((0, 0), (0, META - meta.shape[1]))).astype(BF16)
    tokens = hidden.reshape(rows, model_dim)
    half = model_dim // 2
    experts = jnp.stack([my_index, my_index ^ 1]).astype(F32)
    mixed = moe(
        experts,
        jnp.concatenate([tokens[:, :half], meta], axis=1),
        tokens,
        w_gate_up[0],
        w_down[0],
    )
    relocated = relocate(swap_step, w_down[0], other_down)
    return (mixed.reshape(hidden.shape), relocated[None])


def solution(mesh):
    in_specs = (
        P(None, ("dp", "ep"), None),
        P(None, ("dp", "ep"), None),
        P(None, ("dp", "ep"), None),
        P("ep", None, None),
        P("ep", None, None),
        P("dp"),
    )
    out_specs = (P(None, ("dp", "ep"), None), P(("dp", "ep"), None, None))
    return jax.shard_map(
        on_device, mesh=mesh, in_specs=in_specs, out_specs=out_specs, check_vma=False
    )
```
